32 devices in a mesh: ctx: 8 (over z, y), head: 4 (over x, core).
Axes of the slice: x: 2, y: 2, z: 4, core: 2. Of those that a mesh axis runs over, the one named last changes fastest.
Arguments:
- q_nope: bfloat16 [2048, 16384], P('ctx', 'head'), may hold values from -4 to 4
- q_rope: bfloat16 [2048, 8192], P('ctx', 'head'), may hold values from -8 to 8
- kv_latent: bfloat16 [2048, 576], P(('ctx', 'head')), may hold values from -6 to 6
- half_order: int32 [16], replicated, may hold values from 0 to 15, as said below
- w_uk: bfloat16 [128, 128, 512], P('head'), may hold values from -0.5 to 0.5
- w_uv: bfloat16 [128, 512, 128], P('head'), may hold values from -1.5 to 1.5
Outputs:
- attended: bfloat16 [2048, 16384], P('ctx', 'head')
The draws below stay inside these ranges and needn't reach their ends.
Inputs may be any that keep to these rules, and one draw needn't show every extreme that they name: `half_order`: a permutation of 0 to 15.
All inputs are finite; a program needn't handle non-finite values.
Results may differ from the reference program's by a relative error of at most 0.0085.
Values may be sent and summed in bfloat16 or wider, within the bound.
A program may use at most 128 MiB of HBM per device.

```python
import jax
import jax.numpy as jnp
from jax import lax

HEADS = 128
LATENT = 512
ROPE = 64
NOPE = 128
VDIM = 128
TOKENS = 2048
HALVES = 16


def order_of(key):
    return jax.random.permutation(jax.random.fold_in(key, 11), HALVES).astype(jnp.int32)


def draw_half_order(key, part):
    return order_of(key)


def draw_q_rope(key, part):
    inner_key = jax.random.fold_in(key, 31)
    base = jnp.clip(jax.random.normal(inner_key, (TOKENS, HEADS, ROPE), jnp.float32), -4.0, 4.0)
    return base.reshape(TOKENS, HEADS * ROPE).astype(jnp.bfloat16)


def draw_kv_latent(key, part):
    inner_key = jax.random.fold_in(key, 41)
    base = jnp.clip(jax.random.normal(inner_key, (TOKENS, LATENT + ROPE), jnp.float32), -4.0, 4.0)
    return base.astype(jnp.bfloat16)


def levels(own_key, extent, shards, smallest, top_value):
    def one(dim, parts):
        draws = jax.random.uniform(jax.random.fold_in(jax.random.fold_in(own_key, 6), dim), (parts,), jnp.float32, smallest / len(shards), top_value / len(shards))
        return jnp.repeat(jnp.exp(draws), extent[dim] // parts).reshape((-1,) + (1,) * (len(extent) - dim - 1))

    loudness = one(*shards[0])
    for cut in shards[1:]:
        loudness = loudness * one(*cut)
    return loudness


def noise(rng, dims, deviation, most, cuts=(), kind=jnp.bfloat16):
    drawn = deviation * jax.random.normal(rng, dims, jnp.float32)
    if cuts:
        drawn = drawn * levels(rng, dims, cuts, -0.22, 0.18)
    return jnp.clip(drawn, -most, most).astype(kind)


def setup_inputs(seed: int = 0) -> dict:
    arg_keys = jax.random.split(jax.random.key(seed), 7)
    return {
        "q_nope": noise(arg_keys[0], (TOKENS, HEADS * NOPE), 1.0, 4.0, ((0, 8), (1, 4))),
        "q_rope": draw_q_rope(jax.random.fold_in(arg_keys[6], 71), 0),
        "kv_latent": draw_kv_latent(jax.random.fold_in(arg_keys[6], 71), 0),
        "half_order": draw_half_order(jax.random.fold_in(arg_keys[6], 71), 0),
        "w_uk": noise(arg_keys[4], (HEADS, NOPE, LATENT), NOPE ** -0.5, 0.5, ((0, 4),)),
        "w_uv": noise(arg_keys[5], (HEADS, LATENT, VDIM), (LATENT // 32) ** -0.5, 1.5, ((0, 4),)),
    }


def reference(q_nope, q_rope, kv_latent, half_order, w_uk, w_uv):
    head_count, nope_width, latent_width = w_uk.shape
    value_width = w_uv.shape[2]
    token_count = q_nope.shape[0]
    rope_width = q_rope.shape[1] // head_count
    half_rows = token_count // half_order.shape[0]
    index_rows = jnp.arange(token_count, dtype=jnp.int32)
    position = half_order[index_rows // half_rows] * half_rows + index_rows % half_rows
    visible = position[None, :] <= position[:, None]
    key_latent = kv_latent[:, :latent_width].astype(jnp.float32)
    key_rope = kv_latent[:, latent_width:].astype(jnp.float32)
    score_scale = (nope_width + rope_width) ** -0.5
    queries = q_nope.reshape(token_count, head_count, nope_width).transpose(1, 0, 2)
    query_rope = q_rope.reshape(token_count, head_count, rope_width).transpose(1, 0, 2)

    def one_head(operands):
        query_head, rope_head, key_weight, value_weight = operands
        query_latent = jnp.dot(query_head.astype(jnp.float32), key_weight.astype(jnp.float32)).astype(jnp.bfloat16)
        scores = jnp.dot(query_latent.astype(jnp.float32), key_latent.T) + jnp.dot(rope_head.astype(jnp.float32), key_rope.T)
        scores = scores * score_scale
        masked = jnp.where(visible, scores, -1e30)
        row_max = jnp.max(masked, axis=1, keepdims=True)
        weights = jnp.where(visible, jnp.exp(jnp.minimum(scores - row_max, 0.0)), 0.0)
        weight_sum = jnp.sum(weights, axis=1, keepdims=True)
        summed = jnp.dot(weights.astype(jnp.bfloat16).astype(jnp.float32), key_latent)
        out_latent = (summed / weight_sum).astype(jnp.bfloat16)
        return jnp.dot(out_latent.astype(jnp.float32), value_weight.astype(jnp.float32)).astype(jnp.bfloat16)

    outputs = lax.map(one_head, (queries, query_rope, w_uk, w_uv))
    return outputs.transpose(1, 0, 2).reshape(token_count, head_count * value_width)
```

```python
import functools
import math

import jax
import jax.numpy as jnp
from jax import lax
from jax.experimental import pallas as pl
from jax.experimental.pallas import tpu as pltpu
from jax.sharding import PartitionSpec as P

LANES = 128


def attend_kernel(
    scale,
    tiles,
    group,
    latent_width,
    half_pos,
    own_pos,
    q_ref,
    rope_ref,
    kv_ref,
    w_uk_ref,
    w_uv_ref,
    out_ref,
    keys,
    q_tile,
    scores_even,
    scores_odd,
    peak_even,
    peak_odd,
    weight_sum,
    total,
):
    half = pl.program_id(0)
    tile = pl.program_id(1)
    half_rows = q_ref.shape[0]
    rows = group * half_rows
    per_half = half_rows // LANES
    nope_width = w_uk_ref.shape[1]
    value_width = w_uv_ref.shape[2]
    rope_width = rope_ref.shape[1] // group
    halves = keys.shape[0] // half_rows
    own = own_pos[half]
    wide = 4
    full = own // wide
    left = own + 1 - full * wide

    @pl.when((half == 0) & (tile == 0))
    def _():
        for block in range(halves):
            start = pl.multiple_of(half_pos[block] * half_rows, half_rows)
            keys[pl.ds(start, half_rows), :] = kv_ref[block * half_rows : (block + 1) * half_rows, :]

    def block_of(start_half, count, masked, to_scores, to_peak, from_scores, shift):
        start = pl.multiple_of(start_half * half_rows, half_rows)
        block = keys[pl.ds(start, count * half_rows), :]
        chunk = start_half * per_half
        chunks = count * per_half
        if from_scores is not None:
            parts = []
            added = weight_sum[...]
            for c in range(chunks):
                part = jnp.exp2((from_scores[chunk + c] - shift) * scale)
                added = added + part
                parts.append(part.astype(jnp.bfloat16))
            weight_sum[...] = added
            total[...] += jnp.dot(
                jnp.concatenate(parts, axis=1), block[:, :latent_width], preferred_element_type=jnp.float32
            )
        if to_scores is not None:
            scores = lax.dot_general(
                q_tile[...], block, (((1,), (1,)), ((), ())), preferred_element_type=jnp.float32
            )
            peak = to_peak[...]
            for c in range(chunks):
                part = scores[:, c * LANES : (c + 1) * LANES]
                if masked:
                    query = lax.broadcasted_iota(jnp.int32, (rows, LANES), 0) % half_rows
                    key = lax.broadcasted_iota(jnp.int32, (rows, LANES), 1)
                    part = jnp.where(key - query <= own * half_rows - start - c * LANES, part, -1e30)
                to_scores[chunk + c] = part
                peak = jnp.maximum(peak, part)
            to_peak[...] = peak

    def run(to_scores, to_peak, from_scores, from_peak):
        shift = None
        if to_scores is not None:
            for head in range(group):
                lat = jnp.dot(
                    q_ref[:, head * nope_width : (head + 1) * nope_width],
                    w_uk_ref[head],
                    preferred_element_type=jnp.float32,
                )
                q_tile[head * half_rows : (head + 1) * half_rows, :latent_width] = lat.astype(jnp.bfloat16)
                q_tile[head * half_rows : (head + 1) * half_rows, latent_width:] = rope_ref[
                    :, head * rope_width : (head + 1) * rope_width
                ]
            to_peak[...] = jnp.full_like(to_peak, -1e30)
        if from_scores is not None:
            from_peak[...] = jnp.broadcast_to(jnp.max(from_peak[...], axis=1, keepdims=True), from_peak.shape)
            weight_sum[...] = jnp.zeros_like(weight_sum)
            total[...] = jnp.zeros_like(total)

        def visit(start_half, count, masked):
            shift = None if from_peak is None else from_peak[...]
            block_of(start_half, count, masked, to_scores, to_peak, from_scores, shift)

        @pl.loop(0, full)
        def _(turn):
            visit(turn * wide, wide, False)

        @pl.when(left <= wide // 2)
        def _():
            visit(full * wide, wide // 2, True)

        @pl.when(left > wide // 2)
        def _():
            visit(full * wide, wide, True)

        if from_scores is not None:
            den = jnp.sum(weight_sum[...], axis=1, keepdims=True)
            lat = (total[...] / den).astype(jnp.bfloat16)
            for head in range(group):
                value = jnp.dot(
                    lat[head * half_rows : (head + 1) * half_rows],
                    w_uv_ref[head],
                    preferred_element_type=jnp.float32,
                )
                out_ref[:, head * value_width : (head + 1) * value_width] = value.astype(out_ref.dtype)

    even = (scores_even, peak_even)
    odd = (scores_odd, peak_odd)
    none = (None, None)
    last = even if tiles % 2 == 1 else odd

    @pl.when(tile == 0)
    def _():
        run(*even, *none)

    @pl.when((tile > 0) & (tile < tiles) & (tile % 2 == 1))
    def _():
        run(*odd, *even)

    @pl.when((tile > 0) & (tile < tiles) & (tile % 2 == 0))
    def _():
        run(*even, *odd)

    @pl.when(tile == tiles)
    def _():
        run(*none, *last)


def attend(q_nope, q_rope, kv, half_order, own_pos, w_uk, w_uv):
    heads, nope_width, latent_width = w_uk.shape
    value_width = w_uv.shape[2]
    query_rows = q_nope.shape[0]
    rope_width = q_rope.shape[1] // heads
    key_rows = kv.shape[0]
    half_rows = key_rows // half_order.shape[0]
    group = 2
    tiles = heads // group
    rows = group * half_rows
    scale = (nope_width + rope_width) ** (-0.5) * math.log2(math.e)
    ahead = lambda tile: jnp.minimum(tile, tiles - 1)
    behind = lambda tile: jnp.maximum(tile - 1, 0)
    scores = pltpu.VMEM((key_rows // LANES, rows, LANES), jnp.float32)
    lanes = pltpu.VMEM((rows, LANES), jnp.float32)
    return pl.pallas_call(
        functools.partial(attend_kernel, scale, tiles, group, latent_width),
        out_shape=jax.ShapeDtypeStruct((query_rows, heads * value_width), jnp.bfloat16),
        grid_spec=pltpu.PrefetchScalarGridSpec(
            num_scalar_prefetch=2,
            grid=(query_rows // half_rows, tiles + 1),
            in_specs=[
                pl.BlockSpec((half_rows, group * nope_width), lambda b, t, *_: (b, ahead(t))),
                pl.BlockSpec((half_rows, group * rope_width), lambda b, t, *_: (b, ahead(t))),
                pl.BlockSpec(kv.shape, lambda b, t, *_: (0, 0), pipeline_mode=pl.Buffered(1)),
                pl.BlockSpec((group, nope_width, latent_width), lambda b, t, *_: (ahead(t), 0, 0)),
                pl.BlockSpec((group, latent_width, value_width), lambda b, t, *_: (behind(t), 0, 0)),
            ],
            out_specs=pl.BlockSpec((half_rows, group * value_width), lambda b, t, *_: (b, behind(t))),
            scratch_shapes=[
                pltpu.VMEM(kv.shape, jnp.bfloat16),
                pltpu.VMEM((rows, kv.shape[1]), jnp.bfloat16),
                scores,
                scores,
                lanes,
                lanes,
                lanes,
                pltpu.VMEM((rows, latent_width), jnp.float32),
            ],
        ),
        compiler_params=pltpu.CompilerParams(
            dimension_semantics=("arbitrary", "arbitrary"), vmem_limit_bytes=60 * 1024 * 1024
        ),
        name="attend",
    )(half_order, own_pos, q_nope, q_rope, kv, w_uk, w_uv)


def on_device(q_nope, q_rope, kv_latent, half_order, w_uk, w_uv):
    kv = lax.all_gather(kv_latent, ("ctx", "head"), axis=0, tiled=True)
    half_rows = kv.shape[0] // half_order.shape[0]
    own_halves = q_nope.shape[0] // half_rows
    own_pos = lax.dynamic_slice_in_dim(half_order, lax.axis_index("ctx") * own_halves, own_halves)
    return attend(q_nope, q_rope, kv, half_order, own_pos, w_uk, w_uv)


def solution(mesh):
    return jax.shard_map(
        on_device,
        mesh=mesh,
        in_specs=(
            P("ctx", "head"),
            P("ctx", "head"),
            P(("ctx", "head"), None),
            P(),
            P("head", None, None),
            P("head", None, None),
        ),
        out_specs=P("ctx", "head"),
        check_vma=False,
    )
```

```python
import functools
import math

import jax
import jax.numpy as jnp
from jax import lax
from jax.experimental import pallas as pl
from jax.experimental.pallas import tpu as pltpu
from jax.sharding import PartitionSpec as P

LANES = 128


def flipped(index, bit):
    return index + bit * (1 - 2 * ((index // bit) % 2))


def hop_orders(ctx_size, head_size, pieces):
    base = [("ctx", 1 << k) for k in reversed(range(ctx_size.bit_length() - 1))]
    base += [("head", 1 << k) for k in reversed(range(1, head_size.bit_length() - 1))]
    if len(base) < 4:
        return [base] * pieces
    orders = [
        base,
        base[:-2] + [base[-1], base[-2]],
        [base[-2], base[0], base[-1]] + base[1:-2],
        [base[0], base[-1]] + base[1:-2] + [base[-2]],
    ]
    return [orders[piece % 4] for piece in range(pieces)]


def slot_mask(order, slot, head_size):
    hops = order + [("head", 1)]
    taken = [hop for k, hop in enumerate(hops) if (slot >> k) & 1]
    return sum(bit * (head_size if axis == "ctx" else 1) for axis, bit in taken)


def gather_kernel(orders, kv_ref, out_ref, own_sem, send_sem, recv_sem, core_send_sem, core_recv_sem):
    place = {"ctx": lax.axis_index("ctx"), "head": lax.axis_index("head")}
    pieces, slots, piece_rows, _ = out_ref.shape
    hops = len(orders[0])

    def partner(axis, bit):
        return {**place, axis: flipped(place[axis], bit)}

    own = []
    for piece in range(pieces):
        rows = kv_ref.at[pl.ds(piece * piece_rows, piece_rows), :]
        own.append(pltpu.make_async_copy(rows, out_ref.at[piece, 0], own_sem.at[piece]))
        own[-1].start()
    barrier = pltpu.get_barrier_semaphore()
    greeted = sorted(orders[0]) + [("head", 1)]
    for axis, bit in greeted:
        pl.semaphore_signal(barrier, inc=1, device_id=partner(axis, bit), device_id_type=pl.DeviceIdType.MESH)
    pl.semaphore_wait(barrier, len(greeted))

    def hop(piece, k):
        size = 1 << k
        return pltpu.make_async_remote_copy(
            src_ref=out_ref.at[piece, pl.ds(0, size)],
            dst_ref=out_ref.at[piece, pl.ds(size, size)],
            send_sem=send_sem.at[piece, k],
            recv_sem=recv_sem.at[piece, k],
            device_id=partner(*orders[piece][k]),
            device_id_type=pl.DeviceIdType.MESH,
        )

    def across(piece, k):
        start, size = (0, 1) if k == 0 else (1 << (k - 1), 1 << (k - 1))
        return pltpu.make_async_remote_copy(
            src_ref=out_ref.at[piece, pl.ds(start, size)],
            dst_ref=out_ref.at[piece, pl.ds(slots // 2 + start, size)],
            send_sem=core_send_sem.at[piece, k],
            recv_sem=core_recv_sem.at[piece, k],
            device_id=partner("head", 1),
            device_id_type=pl.DeviceIdType.MESH,
        )

    for k in range(hops + 1):
        for piece in range(pieces):
            if k == 0:
                own[piece].wait()
            else:
                hop(piece, k - 1).wait_recv()
            if k < hops:
                hop(piece, k).start()
            across(piece, k).start()
    for piece in range(pieces):
        for k in range(hops):
            hop(piece, k).wait_send()
        for k in range(hops + 1):
            across(piece, k).wait()


def gather(kv_latent, orders, devices):
    rows, width = kv_latent.shape
    pieces = len(orders)
    hops = len(orders[0])
    semaphores = pltpu.SemaphoreType.DMA
    return pl.pallas_call(
        functools.partial(gather_kernel, orders),
        out_shape=jax.ShapeDtypeStruct((pieces, devices, rows // pieces, width), kv_latent.dtype),
        in_specs=[pl.BlockSpec(memory_space=pl.ANY)],
        out_specs=pl.BlockSpec(memory_space=pltpu.VMEM),
        scratch_shapes=[
            semaphores((pieces,)),
            semaphores((pieces, hops)),
            semaphores((pieces, hops)),
            semaphores((pieces, hops + 1)),
            semaphores((pieces, hops + 1)),
        ],
        compiler_params=pltpu.CompilerParams(collective_id=0, has_side_effects=True),
        name="gather",
    )(kv_latent)


def attend_kernel(
    scale,
    tiles,
    group,
    latent_width,
    orders,
    head_size,
    half_pos,
    q_ref,
    rope_ref,
    kv_ref,
    w_uk_ref,
    w_uv_ref,
    out_ref,
    keys,
    q_tile,
    scores_even,
    scores_odd,
    peak_even,
    peak_odd,
    weight_sum,
    total,
):
    half = pl.program_id(0)
    tile = pl.program_id(1)
    half_rows = q_ref.shape[0]
    rows = group * half_rows
    per_half = half_rows // LANES
    nope_width = w_uk_ref.shape[1]
    value_width = w_uv_ref.shape[2]
    rope_width = rope_ref.shape[1] // group
    pieces, slots, piece_rows, _ = kv_ref.shape
    ctx_index = lax.axis_index("ctx")
    own = half_pos[ctx_index * pl.num_programs(0) + half]
    wide = 4
    full = own // wide
    left = own + 1 - full * wide

    @pl.when((half == 0) & (tile == 0))
    def _():
        device = ctx_index * head_size + lax.axis_index("head")
        for piece in range(pieces):
            for slot in range(slots):
                source = device ^ slot_mask(orders[piece], slot, head_size)
                row = (source * pieces + piece) * piece_rows
                start = half_pos[row // half_rows] * half_rows + row % half_rows
                keys[pl.ds(pl.multiple_of(start, piece_rows), piece_rows), :] = kv_ref[piece, slot]

    def block_of(start_half, count, masked, to_scores, to_peak, from_scores, shift):
        start = pl.multiple_of(start_half * half_rows, half_rows)
        block = keys[pl.ds(start, count * half_rows), :]
        chunk = start_half * per_half
        chunks = count * per_half
        if from_scores is not None:
            parts = []
            added = weight_sum[...]
            for c in range(chunks):
                part = jnp.exp2((from_scores[chunk + c] - shift) * scale)
                added = added + part
                parts.append(part.astype(jnp.bfloat16))
            weight_sum[...] = added
            total[...] += jnp.dot(
                jnp.concatenate(parts, axis=1), block[:, :latent_width], preferred_element_type=jnp.float32
            )
        if to_scores is not None:
            scores = lax.dot_general(
                q_tile[...], block, (((1,), (1,)), ((), ())), preferred_element_type=jnp.float32
            )
            peak = to_peak[...]
            for c in range(chunks):
                part = scores[:, c * LANES : (c + 1) * LANES]
                if masked:
                    query = lax.broadcasted_iota(jnp.int32, (rows, LANES), 0) % half_rows
                    key = lax.broadcasted_iota(jnp.int32, (rows, LANES), 1)
                    part = jnp.where(key - query <= own * half_rows - start - c * LANES, part, -1e30)
                to_scores[chunk + c] = part
                peak = jnp.maximum(peak, part)
            to_peak[...] = peak

    def run(to_scores, to_peak, from_scores, from_peak):
        shift = None
        if to_scores is not None:
            for head in range(group):
                lat = jnp.dot(
                    q_ref[:, head * nope_width : (head + 1) * nope_width],
                    w_uk_ref[head],
                    preferred_element_type=jnp.float32,
                )
                q_tile[head * half_rows : (head + 1) * half_rows, :latent_width] = lat.astype(jnp.bfloat16)
                q_tile[head * half_rows : (head + 1) * half_rows, latent_width:] = rope_ref[
                    :, head * rope_width : (head + 1) * rope_width
                ]
            to_peak[...] = jnp.full_like(to_peak, -1e30)
        if from_scores is not None:
            from_peak[...] = jnp.broadcast_to(jnp.max(from_peak[...], axis=1, keepdims=True), from_peak.shape)
            weight_sum[...] = jnp.zeros_like(weight_sum)
            total[...] = jnp.zeros_like(total)

        def visit(start_half, count, masked):
            shift = None if from_peak is None else from_peak[...]
            block_of(start_half, count, masked, to_scores, to_peak, from_scores, shift)

        @pl.loop(0, full)
        def _(turn):
            visit(turn * wide, wide, False)

        @pl.when(left <= wide // 2)
        def _():
            visit(full * wide, wide // 2, True)

        @pl.when(left > wide // 2)
        def _():
            visit(full * wide, wide, True)

        if from_scores is not None:
            den = jnp.sum(weight_sum[...], axis=1, keepdims=True)
            lat = (total[...] / den).astype(jnp.bfloat16)
            for head in range(group):
                value = jnp.dot(
                    lat[head * half_rows : (head + 1) * half_rows],
                    w_uv_ref[head],
                    preferred_element_type=jnp.float32,
                )
                out_ref[:, head * value_width : (head + 1) * value_width] = value.astype(out_ref.dtype)

    even = (scores_even, peak_even)
    odd = (scores_odd, peak_odd)
    none = (None, None)
    last = even if tiles % 2 == 1 else odd

    @pl.when(tile == 0)
    def _():
        run(*even, *none)

    @pl.when((tile > 0) & (tile < tiles) & (tile % 2 == 1))
    def _():
        run(*odd, *even)

    @pl.when((tile > 0) & (tile < tiles) & (tile % 2 == 0))
    def _():
        run(*even, *odd)

    @pl.when(tile == tiles)
    def _():
        run(*none, *last)


def attend(q_nope, q_rope, kv, half_order, w_uk, w_uv, orders, head_size):
    heads, nope_width, latent_width = w_uk.shape
    value_width = w_uv.shape[2]
    query_rows = q_nope.shape[0]
    rope_width = q_rope.shape[1] // heads
    key_rows = kv.shape[0] * kv.shape[1] * kv.shape[2]
    half_rows = key_rows // half_order.shape[0]
    group = 2
    tiles = heads // group
    rows = group * half_rows
    scale = (nope_width + rope_width) ** (-0.5) * math.log2(math.e)
    ahead = lambda tile: jnp.minimum(tile, tiles - 1)
    behind = lambda tile: jnp.maximum(tile - 1, 0)
    scores = pltpu.VMEM((key_rows // LANES, rows, LANES), jnp.float32)
    lanes = pltpu.VMEM((rows, LANES), jnp.float32)
    return pl.pallas_call(
        functools.partial(attend_kernel, scale, tiles, group, latent_width, orders, head_size),
        out_shape=jax.ShapeDtypeStruct((query_rows, heads * value_width), jnp.bfloat16),
        grid_spec=pltpu.PrefetchScalarGridSpec(
            num_scalar_prefetch=1,
            grid=(query_rows // half_rows, tiles + 1),
            in_specs=[
                pl.BlockSpec((half_rows, group * nope_width), lambda b, t, *_: (b, ahead(t))),
                pl.BlockSpec((half_rows, group * rope_width), lambda b, t, *_: (b, ahead(t))),
                pl.BlockSpec(kv.shape, lambda b, t, *_: (0, 0, 0, 0), pipeline_mode=pl.Buffered(1)),
                pl.BlockSpec((group, nope_width, latent_width), lambda b, t, *_: (ahead(t), 0, 0)),
                pl.BlockSpec((group, latent_width, value_width), lambda b, t, *_: (behind(t), 0, 0)),
            ],
            out_specs=pl.BlockSpec((half_rows, group * value_width), lambda b, t, *_: (b, behind(t))),
            scratch_shapes=[
                pltpu.VMEM((key_rows, kv.shape[3]), jnp.bfloat16),
                pltpu.VMEM((rows, kv.shape[3]), jnp.bfloat16),
                scores,
                scores,
                lanes,
                lanes,
                lanes,
                pltpu.VMEM((rows, latent_width), jnp.float32),
            ],
        ),
        compiler_params=pltpu.CompilerParams(
            dimension_semantics=("arbitrary", "arbitrary"), vmem_limit_bytes=60 * 1024 * 1024
        ),
        name="attend",
    )(half_order, q_nope, q_rope, kv, w_uk, w_uv)


def on_device(ctx_size, head_size, q_nope, q_rope, kv_latent, half_order, w_uk, w_uv):
    pieces = max(1, min(4, kv_latent.shape[0] // 16))
    orders = hop_orders(ctx_size, head_size, pieces)
    kv = gather(kv_latent, orders, ctx_size * head_size)
    return attend(q_nope, q_rope, kv, half_order, w_uk, w_uv, orders, head_size)


def solution(mesh):
    return jax.shard_map(
        functools.partial(on_device, mesh.shape["ctx"], mesh.shape["head"]),
        mesh=mesh,
        in_specs=(
            P("ctx", "head"),
            P("ctx", "head"),
            P(("ctx", "head"), None),
            P(),
            P("head", None, None),
            P("head", None, None),
        ),
        out_specs=P("ctx", "head"),
        check_vma=False,
    )
```

```python
import functools
import math

import jax
import jax.numpy as jnp
from jax import lax
from jax.experimental import pallas as pl
from jax.experimental.pallas import tpu as pltpu
from jax.sharding import PartitionSpec as P

LANES = 128


def flipped(index, bit):
    return index + bit * (1 - 2 * ((index // bit) % 2))


def hop_orders(ctx_size, head_size, pieces):
    base = [("ctx", 1 << k) for k in reversed(range(ctx_size.bit_length() - 1))]
    base += [("head", 1 << k) for k in reversed(range(1, head_size.bit_length() - 1))]
    if len(base) < 4:
        return [base] * pieces
    orders = [
        base,
        base[:-2] + [base[-1], base[-2]],
        [base[-2], base[0], base[-1]] + base[1:-2],
        [base[0], base[-1]] + base[1:-2] + [base[-2]],
    ]
    return [orders[piece % 4] for piece in range(pieces)]


def slot_mask(order, slot, head_size):
    hops = order + [("head", 1)]
    taken = [hop for k, hop in enumerate(hops) if (slot >> k) & 1]
    return sum(bit * (head_size if axis == "ctx" else 1) for axis, bit in taken)


def gather_kernel(orders, kv_ref, out_ref, own_sem, send_sem, recv_sem, core_send_sem, core_recv_sem):
    place = {"ctx": lax.axis_index("ctx"), "head": lax.axis_index("head")}
    pieces, slots, piece_rows, _ = out_ref.shape
    hops = len(orders[0])

    def partner(axis, bit):
        return {**place, axis: flipped(place[axis], bit)}

    own = []
    for piece in range(pieces):
        rows = kv_ref.at[pl.ds(piece * piece_rows, piece_rows), :]
        own.append(pltpu.make_async_copy(rows, out_ref.at[piece, 0], own_sem.at[piece]))
        own[-1].start()
    barrier = pltpu.get_barrier_semaphore()
    greeted = sorted(orders[0]) + [("head", 1)]
    for axis, bit in greeted:
        pl.semaphore_signal(barrier, inc=1, device_id=partner(axis, bit), device_id_type=pl.DeviceIdType.MESH)
    pl.semaphore_wait(barrier, len(greeted))

    def hop(piece, k):
        size = 1 << k
        return pltpu.make_async_remote_copy(
            src_ref=out_ref.at[piece, pl.ds(0, size)],
            dst_ref=out_ref.at[piece, pl.ds(size, size)],
            send_sem=send_sem.at[piece, k],
            recv_sem=recv_sem.at[piece, k],
            device_id=partner(*orders[piece][k]),
            device_id_type=pl.DeviceIdType.MESH,
        )

    def across(piece, k):
        start, size = (0, 1) if k == 0 else (1 << (k - 1), 1 << (k - 1))
        return pltpu.make_async_remote_copy(
            src_ref=out_ref.at[piece, pl.ds(start, size)],
            dst_ref=out_ref.at[piece, pl.ds(slots // 2 + start, size)],
            send_sem=core_send_sem.at[piece, k],
            recv_sem=core_recv_sem.at[piece, k],
            device_id=partner("head", 1),
            device_id_type=pl.DeviceIdType.MESH,
        )

    for k in range(hops + 1):
        for piece in range(pieces):
            if k == 0:
                own[piece].wait()
            else:
                hop(piece, k - 1).wait_recv()
            if k < hops:
                hop(piece, k).start()
            across(piece, k).start()
    for piece in range(pieces):
        for k in range(hops):
            hop(piece, k).wait_send()
        for k in range(hops + 1):
            across(piece, k).wait()


def gather(kv_latent, orders, devices):
    rows, width = kv_latent.shape
    pieces = len(orders)
    hops = len(orders[0])
    semaphores = pltpu.SemaphoreType.DMA
    return pl.pallas_call(
        functools.partial(gather_kernel, orders),
        out_shape=jax.ShapeDtypeStruct((pieces, devices, rows // pieces, width), kv_latent.dtype),
        in_specs=[pl.BlockSpec(memory_space=pl.ANY)],
        out_specs=pl.BlockSpec(memory_space=pltpu.VMEM),
        scratch_shapes=[
            semaphores((pieces,)),
            semaphores((pieces, hops)),
            semaphores((pieces, hops)),
            semaphores((pieces, hops + 1)),
            semaphores((pieces, hops + 1)),
        ],
        compiler_params=pltpu.CompilerParams(collective_id=0, has_side_effects=True),
        name="gather",
    )(kv_latent)


def attend_kernel(
    scale,
    tiles,
    group,
    latent_width,
    orders,
    head_size,
    half_pos,
    q_ref,
    rope_ref,
    kv_ref,
    w_uk_ref,
    w_uv_ref,
    out_ref,
    keys,
    q_tile,
    scores_even,
    scores_odd,
    peak_even,
    peak_odd,
    weight_sum,
    total,
):
    half = pl.program_id(0)
    tile = pl.program_id(1)
    half_rows = q_ref.shape[0]
    rows = group * half_rows
    per_half = half_rows // LANES
    nope_width = w_uk_ref.shape[1]
    value_width = w_uv_ref.shape[2]
    rope_width = rope_ref.shape[1] // group
    pieces, slots, piece_rows, _ = kv_ref.shape
    ctx_index = lax.axis_index("ctx")
    own = half_pos[ctx_index * pl.num_programs(0) + half]
    wide = 4
    full = own // wide
    left = own + 1 - full * wide

    @pl.when((half == 0) & (tile == 0))
    def _():
        device = ctx_index * head_size + lax.axis_index("head")
        for piece in range(pieces):
            for slot in range(slots):
                source = device ^ slot_mask(orders[piece], slot, head_size)
                row = (source * pieces + piece) * piece_rows
                start = half_pos[row // half_rows] * half_rows + row % half_rows
                keys[pl.ds(pl.multiple_of(start, piece_rows), piece_rows), :] = kv_ref[piece, slot]

    def block_of(start_half, count, masked, to_scores, to_peak, from_scores, shift):
        start = pl.multiple_of(start_half * half_rows, half_rows)
        block = keys[pl.ds(start, count * half_rows), :]
        chunk = start_half * per_half
        chunks = count * per_half
        if from_scores is not None:
            parts = []
            added = weight_sum[...]
            for c in range(chunks):
                part = jnp.exp2((from_scores[chunk + c] - shift) * scale)
                added = added + part
                parts.append(part.astype(jnp.bfloat16))
            weight_sum[...] = added
            total[...] += jnp.dot(
                jnp.concatenate(parts, axis=1), block[:, :latent_width], preferred_element_type=jnp.float32
            )
        if to_scores is not None:
            scores = lax.dot_general(
                q_tile[...], block, (((1,), (1,)), ((), ())), preferred_element_type=jnp.float32
            )
            peak = to_peak[...]
            for c in range(chunks):
                part = scores[:, c * LANES : (c + 1) * LANES]
                if masked:
                    query = lax.broadcasted_iota(jnp.int32, (rows, LANES), 0) % half_rows
                    key = lax.broadcasted_iota(jnp.int32, (rows, LANES), 1)
                    part = jnp.where(key - query <= own * half_rows - start - c * LANES, part, -1e30)
                to_scores[chunk + c] = part
                peak = jnp.maximum(peak, part)
            to_peak[...] = peak

    def run(to_scores, to_peak, from_scores, from_peak):
        shift = None
        if to_scores is not None:
            for head in range(group):
                lat = jnp.dot(
                    q_ref[:, head * nope_width : (head + 1) * nope_width],
                    w_uk_ref[head],
                    preferred_element_type=jnp.float32,
                )
                q_tile[head * half_rows : (head + 1) * half_rows, :latent_width] = lat.astype(jnp.bfloat16)
                q_tile[head * half_rows : (head + 1) * half_rows, latent_width:] = rope_ref[
                    :, head * rope_width : (head + 1) * rope_width
                ]
            to_peak[...] = jnp.full_like(to_peak, -1e30)
        if from_scores is not None:
            from_peak[...] = jnp.broadcast_to(jnp.max(from_peak[...], axis=1, keepdims=True), from_peak.shape)
            weight_sum[...] = jnp.zeros_like(weight_sum)
            total[...] = jnp.zeros_like(total)

        def visit(start_half, count, masked):
            shift = None if from_peak is None else from_peak[...]
            block_of(start_half, count, masked, to_scores, to_peak, from_scores, shift)

        @pl.loop(0, full)
        def _(turn):
            visit(turn * wide, wide, False)

        @pl.when(left <= wide // 2)
        def _():
            visit(full * wide, wide // 2, True)

        @pl.when(left > wide // 2)
        def _():
            visit(full * wide, wide, True)

        if from_scores is not None:
            den = jnp.sum(weight_sum[...], axis=1, keepdims=True)
            lat = (total[...] / den).astype(jnp.bfloat16)
            for head in range(group):
                value = jnp.dot(
                    lat[head * half_rows : (head + 1) * half_rows],
                    w_uv_ref[head],
                    preferred_element_type=jnp.float32,
                )
                out_ref[:, head * value_width : (head + 1) * value_width] = value.astype(out_ref.dtype)

    even = (scores_even, peak_even)
    odd = (scores_odd, peak_odd)
    none = (None, None)
    last = even if tiles % 2 == 1 else odd

    @pl.when(tile == 0)
    def _():
        run(*even, *none)

    @pl.when((tile > 0) & (tile < tiles) & (tile % 2 == 1))
    def _():
        run(*odd, *even)

    @pl.when((tile > 0) & (tile < tiles) & (tile % 2 == 0))
    def _():
        run(*even, *odd)

    @pl.when(tile == tiles)
    def _():
        run(*none, *last)


def attend(q_nope, q_rope, kv, half_order, w_uk, w_uv, orders, head_size):
    heads, nope_width, latent_width = w_uk.shape
    value_width = w_uv.shape[2]
    query_rows = q_nope.shape[0]
    rope_width = q_rope.shape[1] // heads
    key_rows = kv.shape[0] * kv.shape[1] * kv.shape[2]
    half_rows = key_rows // half_order.shape[0]
    group = math.gcd(heads, 8)
    tiles = heads // group
    rows = group * half_rows
    scale = (nope_width + rope_width) ** (-0.5) * math.log2(math.e)
    ahead = lambda tile: jnp.minimum(tile, tiles - 1)
    behind = lambda tile: jnp.maximum(tile - 1, 0)
    scores = pltpu.VMEM((key_rows // LANES, rows, LANES), jnp.float32)
    lanes = pltpu.VMEM((rows, LANES), jnp.float32)
    return pl.pallas_call(
        functools.partial(attend_kernel, scale, tiles, group, latent_width, orders, head_size),
        out_shape=jax.ShapeDtypeStruct((query_rows, heads * value_width), jnp.bfloat16),
        grid_spec=pltpu.PrefetchScalarGridSpec(
            num_scalar_prefetch=1,
            grid=(query_rows // half_rows, tiles + 1),
            in_specs=[
                pl.BlockSpec((half_rows, group * nope_width), lambda b, t, *_: (b, ahead(t))),
                pl.BlockSpec((half_rows, group * rope_width), lambda b, t, *_: (b, ahead(t))),
                pl.BlockSpec(kv.shape, lambda b, t, *_: (0, 0, 0, 0), pipeline_mode=pl.Buffered(1)),
                pl.BlockSpec((group, nope_width, latent_width), lambda b, t, *_: (ahead(t), 0, 0)),
                pl.BlockSpec((group, latent_width, value_width), lambda b, t, *_: (behind(t), 0, 0)),
            ],
            out_specs=pl.BlockSpec((half_rows, group * value_width), lambda b, t, *_: (b, behind(t))),
            scratch_shapes=[
                pltpu.VMEM((key_rows, kv.shape[3]), jnp.bfloat16),
                pltpu.VMEM((rows, kv.shape[3]), jnp.bfloat16),
                scores,
                scores,
                lanes,
                lanes,
                lanes,
                pltpu.VMEM((rows, latent_width), jnp.float32),
            ],
        ),
        compiler_params=pltpu.CompilerParams(
            dimension_semantics=("arbitrary", "arbitrary"), vmem_limit_bytes=60 * 1024 * 1024
        ),
        name="attend",
    )(half_order, q_nope, q_rope, kv, w_uk, w_uv)


def on_device(ctx_size, head_size, q_nope, q_rope, kv_latent, half_order, w_uk, w_uv):
    pieces = max(1, min(4, kv_latent.shape[0] // 16))
    orders = hop_orders(ctx_size, head_size, pieces)
    kv = gather(kv_latent, orders, ctx_size * head_size)
    return attend(q_nope, q_rope, kv, half_order, w_uk, w_uv, orders, head_size)


def solution(mesh):
    return jax.shard_map(
        functools.partial(on_device, mesh.shape["ctx"], mesh.shape["head"]),
        mesh=mesh,
        in_specs=(
            P("ctx", "head"),
            P("ctx", "head"),
            P(("ctx", "head"), None),
            P(),
            P("head", None, None),
            P("head", None, None),
        ),
        out_specs=P("ctx", "head"),
        check_vma=False,
    )
```

```python
import functools
import math

import jax
import jax.numpy as jnp
from jax import lax
from jax.experimental import pallas as pl
from jax.experimental.pallas import tpu as pltpu
from jax.sharding import PartitionSpec as P

LANES = 128


def flipped(index, bit):
    return index + bit * (1 - 2 * ((index // bit) % 2))


def hop_orders(ctx_size, head_size, pieces):
    base = [("ctx", 1 << k) for k in reversed(range(ctx_size.bit_length() - 1))]
    base += [("head", 1 << k) for k in reversed(range(1, head_size.bit_length() - 1))]
    if len(base) < 4:
        return [base] * pieces
    orders = [
        base,
        base[:-2] + [base[-1], base[-2]],
        [base[-2], base[0], base[-1]] + base[1:-2],
        [base[0], base[-1]] + base[1:-2] + [base[-2]],
    ]
    return [orders[piece % 4] for piece in range(pieces)]


def slot_mask(order, slot, head_size):
    hops = order + [("head", 1)]
    taken = [hop for k, hop in enumerate(hops) if (slot >> k) & 1]
    return sum(bit * (head_size if axis == "ctx" else 1) for axis, bit in taken)


def gather_kernel(orders, kv_ref, out_ref, own_sem, send_sem, recv_sem, core_send_sem, core_recv_sem):
    place = {"ctx": lax.axis_index("ctx"), "head": lax.axis_index("head")}
    pieces, slots, piece_rows, _ = out_ref.shape
    hops = len(orders[0])

    def partner(axis, bit):
        return {**place, axis: flipped(place[axis], bit)}

    own = []
    for piece in range(pieces):
        rows = kv_ref.at[pl.ds(piece * piece_rows, piece_rows), :]
        own.append(pltpu.make_async_copy(rows, out_ref.at[piece, 0], own_sem.at[piece]))
        own[-1].start()
    barrier = pltpu.get_barrier_semaphore()
    greeted = sorted(orders[0]) + [("head", 1)]
    for axis, bit in greeted:
        pl.semaphore_signal(barrier, inc=1, device_id=partner(axis, bit), device_id_type=pl.DeviceIdType.MESH)
    pl.semaphore_wait(barrier, len(greeted))

    def hop(piece, k):
        size = 1 << k
        return pltpu.make_async_remote_copy(
            src_ref=out_ref.at[piece, pl.ds(0, size)],
            dst_ref=out_ref.at[piece, pl.ds(size, size)],
            send_sem=send_sem.at[piece, k],
            recv_sem=recv_sem.at[piece, k],
            device_id=partner(*orders[piece][k]),
            device_id_type=pl.DeviceIdType.MESH,
        )

    def across(piece, k):
        start, size = (0, 1) if k == 0 else (1 << (k - 1), 1 << (k - 1))
        return pltpu.make_async_remote_copy(
            src_ref=out_ref.at[piece, pl.ds(start, size)],
            dst_ref=out_ref.at[piece, pl.ds(slots // 2 + start, size)],
            send_sem=core_send_sem.at[piece, k],
            recv_sem=core_recv_sem.at[piece, k],
            device_id=partner("head", 1),
            device_id_type=pl.DeviceIdType.MESH,
        )

    for k in range(hops + 1):
        for piece in range(pieces):
            if k == 0:
                own[piece].wait()
            else:
                hop(piece, k - 1).wait_recv()
            if k < hops:
                hop(piece, k).start()
            across(piece, k).start()
    for piece in range(pieces):
        for k in range(hops):
            hop(piece, k).wait_send()
        for k in range(hops + 1):
            across(piece, k).wait()


def gather(kv_latent, orders, devices):
    rows, width = kv_latent.shape
    pieces = len(orders)
    hops = len(orders[0])
    semaphores = pltpu.SemaphoreType.DMA
    return pl.pallas_call(
        functools.partial(gather_kernel, orders),
        out_shape=jax.ShapeDtypeStruct((pieces, devices, rows // pieces, width), kv_latent.dtype),
        in_specs=[pl.BlockSpec(memory_space=pl.ANY)],
        out_specs=pl.BlockSpec(memory_space=pltpu.VMEM),
        scratch_shapes=[
            semaphores((pieces,)),
            semaphores((pieces, hops)),
            semaphores((pieces, hops)),
            semaphores((pieces, hops + 1)),
            semaphores((pieces, hops + 1)),
        ],
        compiler_params=pltpu.CompilerParams(collective_id=0, has_side_effects=True),
        name="gather",
    )(kv_latent)


def attend_kernel(
    scale,
    tiles,
    group,
    latent_width,
    orders,
    head_size,
    half_pos,
    q_ref,
    rope_ref,
    kv_ref,
    w_uk_ref,
    w_uv_ref,
    out_ref,
    keys,
    q_tile,
    scores_even,
    scores_odd,
    peak_even,
    peak_odd,
    weight_sum,
    total,
):
    half = pl.program_id(0)
    tile = pl.program_id(1)
    half_rows = q_ref.shape[0]
    rows = group * half_rows
    per_half = half_rows // LANES
    nope_width = w_uk_ref.shape[1]
    value_width = w_uv_ref.shape[2]
    rope_width = rope_ref.shape[1] // group
    pieces, slots, piece_rows, _ = kv_ref.shape
    ctx_index = lax.axis_index("ctx")
    own = half_pos[ctx_index * pl.num_programs(0) + half]
    wide = 4
    full = own // wide
    left = own + 1 - full * wide

    @pl.when((half == 0) & (tile == 0))
    def _():
        device = ctx_index * head_size + lax.axis_index("head")
        sources = half_rows // (pieces * piece_rows)
        slot_of = [{slot_mask(order, slot, head_size): slot for slot in range(slots)} for order in orders]
        for mask in range(slots):
            source = device ^ mask
            block = lax.div(source, sources)
            first = half_pos[block] * half_rows + (source - block * sources) * pieces * piece_rows
            for piece in range(pieces):
                start = pl.multiple_of(first + piece * piece_rows, piece_rows)
                keys[pl.ds(start, piece_rows), :] = kv_ref[piece, slot_of[piece][mask]]

    def block_of(start_half, count, masked, to_scores, to_peak, from_scores, shift):
        start = pl.multiple_of(start_half * half_rows, half_rows)
        block = keys[pl.ds(start, count * half_rows), :]
        chunk = start_half * per_half
        chunks = count * per_half
        if from_scores is not None:
            parts = []
            added = weight_sum[...]
            for c in range(chunks):
                part = jnp.exp2((from_scores[chunk + c] - shift) * scale)
                added = added + part
                parts.append(part.astype(jnp.bfloat16))
            weight_sum[...] = added
            total[...] += jnp.dot(
                jnp.concatenate(parts, axis=1), block[:, :latent_width], preferred_element_type=jnp.float32
            )
        if to_scores is not None:
            scores = lax.dot_general(
                q_tile[...], block, (((1,), (1,)), ((), ())), preferred_element_type=jnp.float32
            )
            peak = to_peak[...]
            for c in range(chunks):
                part = scores[:, c * LANES : (c + 1) * LANES]
                if masked:
                    query = lax.broadcasted_iota(jnp.int32, (rows, LANES), 0) % half_rows
                    key = lax.broadcasted_iota(jnp.int32, (rows, LANES), 1)
                    part = jnp.where(key - query <= own * half_rows - start - c * LANES, part, -1e30)
                to_scores[chunk + c] = part
                peak = jnp.maximum(peak, part)
            to_peak[...] = peak

    def run(to_scores, to_peak, from_scores, from_peak):
        shift = None
        if to_scores is not None:
            for head in range(group):
                lat = jnp.dot(
                    q_ref[:, head * nope_width : (head + 1) * nope_width],
                    w_uk_ref[head],
                    preferred_element_type=jnp.float32,
                )
                q_tile[head * half_rows : (head + 1) * half_rows, :latent_width] = lat.astype(jnp.bfloat16)
                q_tile[head * half_rows : (head + 1) * half_rows, latent_width:] = rope_ref[
                    :, head * rope_width : (head + 1) * rope_width
                ]
            to_peak[...] = jnp.full_like(to_peak, -1e30)
        if from_scores is not None:
            from_peak[...] = jnp.broadcast_to(jnp.max(from_peak[...], axis=1, keepdims=True), from_peak.shape)
            weight_sum[...] = jnp.zeros_like(weight_sum)
            total[...] = jnp.zeros_like(total)

        def visit(start_half, count, masked):
            shift = None if from_peak is None else from_peak[...]
            block_of(start_half, count, masked, to_scores, to_peak, from_scores, shift)

        @pl.loop(0, full)
        def _(turn):
            visit(turn * wide, wide, False)

        @pl.when(left <= wide // 2)
        def _():
            visit(full * wide, wide // 2, True)

        @pl.when(left > wide // 2)
        def _():
            visit(full * wide, wide, True)

        if from_scores is not None:
            den = jnp.sum(weight_sum[...], axis=1, keepdims=True)
            lat = (total[...] / den).astype(jnp.bfloat16)
            for head in range(group):
                value = jnp.dot(
                    lat[head * half_rows : (head + 1) * half_rows],
                    w_uv_ref[head],
                    preferred_element_type=jnp.float32,
                )
                out_ref[:, head * value_width : (head + 1) * value_width] = value.astype(out_ref.dtype)

    even = (scores_even, peak_even)
    odd = (scores_odd, peak_odd)
    none = (None, None)
    last = even if tiles % 2 == 1 else odd

    @pl.when(tile == 0)
    def _():
        run(*even, *none)

    @pl.when((tile > 0) & (tile < tiles) & (tile % 2 == 1))
    def _():
        run(*odd, *even)

    @pl.when((tile > 0) & (tile < tiles) & (tile % 2 == 0))
    def _():
        run(*even, *odd)

    @pl.when(tile == tiles)
    def _():
        run(*none, *last)


def attend(q_nope, q_rope, kv, half_order, w_uk, w_uv, orders, head_size):
    heads, nope_width, latent_width = w_uk.shape
    value_width = w_uv.shape[2]
    query_rows = q_nope.shape[0]
    rope_width = q_rope.shape[1] // heads
    key_rows = kv.shape[0] * kv.shape[1] * kv.shape[2]
    half_rows = key_rows // half_order.shape[0]
    group = math.gcd(heads, 16)
    tiles = heads // group
    rows = group * half_rows
    scale = (nope_width + rope_width) ** (-0.5) * math.log2(math.e)
    ahead = lambda tile: jnp.minimum(tile, tiles - 1)
    behind = lambda tile: jnp.maximum(tile - 1, 0)
    scores = pltpu.VMEM((key_rows // LANES, rows, LANES), jnp.float32)
    lanes = pltpu.VMEM((rows, LANES), jnp.float32)
    return pl.pallas_call(
        functools.partial(attend_kernel, scale, tiles, group, latent_width, orders, head_size),
        out_shape=jax.ShapeDtypeStruct((query_rows, heads * value_width), jnp.bfloat16),
        grid_spec=pltpu.PrefetchScalarGridSpec(
            num_scalar_prefetch=1,
            grid=(query_rows // half_rows, tiles + 1),
            in_specs=[
                pl.BlockSpec((half_rows, group * nope_width), lambda b, t, *_: (b, ahead(t))),
                pl.BlockSpec((half_rows, group * rope_width), lambda b, t, *_: (b, ahead(t))),
                pl.BlockSpec(kv.shape, lambda b, t, *_: (0, 0, 0, 0), pipeline_mode=pl.Buffered(1)),
                pl.BlockSpec((group, nope_width, latent_width), lambda b, t, *_: (ahead(t), 0, 0)),
                pl.BlockSpec((group, latent_width, value_width), lambda b, t, *_: (behind(t), 0, 0)),
            ],
            out_specs=pl.BlockSpec((half_rows, group * value_width), lambda b, t, *_: (b, behind(t))),
            scratch_shapes=[
                pltpu.VMEM((key_rows, kv.shape[3]), jnp.bfloat16),
                pltpu.VMEM((rows, kv.shape[3]), jnp.bfloat16),
                scores,
                scores,
                lanes,
                lanes,
                lanes,
                pltpu.VMEM((rows, latent_width), jnp.float32),
            ],
        ),
        compiler_params=pltpu.CompilerParams(
            dimension_semantics=("arbitrary", "arbitrary"), vmem_limit_bytes=63 * 1024 * 1024
        ),
        name="attend",
    )(half_order, q_nope, q_rope, kv, w_uk, w_uv)


def on_device(ctx_size, head_size, q_nope, q_rope, kv_latent, half_order, w_uk, w_uv):
    pieces = max(1, min(4, kv_latent.shape[0] // 16))
    orders = hop_orders(ctx_size, head_size, pieces)
    kv = gather(kv_latent, orders, ctx_size * head_size)
    return attend(q_nope, q_rope, kv, half_order, w_uk, w_uv, orders, head_size)


def solution(mesh):
    return jax.shard_map(
        functools.partial(on_device, mesh.shape["ctx"], mesh.shape["head"]),
        mesh=mesh,
        in_specs=(
            P("ctx", "head"),
            P("ctx", "head"),
            P(("ctx", "head"), None),
            P(),
            P("head", None, None),
            P("head", None, None),
        ),
        out_specs=P("ctx", "head"),
        check_vma=False,
    )
```
